32 devices in a mesh: dp: 8 (over z, y), section: 4 (over x, core).
Axes of the slice: x: 2, y: 2, z: 4, core: 2. Of those that a mesh axis runs over, the one named last changes fastest.
Arguments:
- hidden_in: bfloat16 [16, 64, 4096], P('dp'), may hold values from -6 to 6
- targets: bfloat16 [16, 64, 4096], P('dp'), may hold values from -6 to 6
- down_factors: bfloat16 [4, 2, 128, 4096], P('section', None, None, 'dp'), may hold values from -0.09375 to 0.09375
- up_factors: bfloat16 [4, 4, 128, 4096], P('section', None, None, 'dp'), may hold values from -18 to 18
- down_dir: bfloat16 [4, 2, 128, 4096], P('section', None, None, 'dp'), may hold values from -0.09375 to 0.09375
- up_dir: bfloat16 [4, 4, 128, 4096], P('section', None, None, 'dp'), may hold values from -0.5 to 0.5
Outputs:
- hv_down: float32 [4, 2, 128, 4096], P('section', None, None, 'dp')
- hv_up: float32 [4, 4, 128, 4096], P('section', None, None, 'dp')
The draws below stay inside these ranges and needn't reach their ends.
All inputs are finite; a program needn't handle non-finite values.
Results may differ from the reference program's by a relative error of at most 0.025.
Values may be sent and summed in bfloat16 or wider, within the bound.
No kernel may reach another device: no remote copies, remote signals or barrier semaphores. Data moves between devices by JAX's collectives and lax.ppermute only.
A program may use at most 192 MiB of HBM per device.

```python
import math
import jax
import jax.numpy as jnp
from jax import lax

D = 4096
HEAD_DIM = 128
RANK = 128
TOK = 64
MICRO = 2
SECTIONS = 4
SEQS = 16
N_DP = 8


def draw_up_factors(key, part):
    base = jax.random.truncated_normal(key, -6.0, 6.0, (SECTIONS, 4, RANK, D), jnp.float32) * RANK ** (-0.5)
    return base.astype(jnp.bfloat16)


def shard_levels(own_key, extent, pieces, low, high):
    gain, own = 1.0, jax.random.fold_in(own_key, 6)
    for axis_at, shards_of in pieces:
        heights = jnp.exp(jax.random.uniform(jax.random.fold_in(own, axis_at), (shards_of,), jnp.float32, low / len(pieces), high / len(pieces)))
        gain = gain * jnp.repeat(heights, extent[axis_at] // shards_of).reshape([-1 if axis == axis_at else 1 for axis in range(len(extent))])
    return gain


def gaussian(rng, shape, scale, most, split=(), kind=jnp.bfloat16):
    entries = jax.random.normal(rng, shape, jnp.float32) * scale
    if len(split) > 0:
        entries = shard_levels(rng, shape, split, -0.22, 0.18) * entries
    return jnp.clip(entries, min=-most, max=most).astype(kind)


def setup_inputs(seed: int = 0) -> dict:
    key_list = jax.random.split(jax.random.key(seed), 7)
    return {
        "hidden_in": gaussian(key_list[0], (SEQS, TOK, D), 1.0, 6.0, ((0, 8),)),
        "targets": gaussian(key_list[1], (SEQS, TOK, D), 1.0, 6.0, ((0, 8),)),
        "down_factors": gaussian(key_list[2], (SECTIONS, 2, RANK, D), D ** -0.5, 0.09375, ((0, 4), (3, 8))),
        "up_factors": draw_up_factors(jax.random.fold_in(key_list[6], 71), 0),
        "down_dir": gaussian(key_list[4], (SECTIONS, 2, RANK, D), D ** -0.5, 0.09375, ((0, 4), (3, 8))),
        "up_dir": gaussian(key_list[5], (SECTIONS, 4, RANK, D), RANK ** -0.5, 0.5, ((0, 4), (3, 8))),
    }


EPS = 1e-05

def layer_step(hidden, down_set, up_set):
    tokens = hidden.shape[0]
    head_count = hidden.shape[1] // HEAD_DIM
    widened = hidden.astype(jnp.float32)
    normed = (widened * lax.rsqrt(lax.optimization_barrier(jnp.mean(widened * widened, axis=-1, keepdims=True)) + EPS)).astype(jnp.bfloat16)
    contract = (((1,), (1,)), ((), ()))
    latent = lax.dot_general(normed, down_set[0], contract, preferred_element_type=jnp.float32).astype(jnp.bfloat16)
    queries = jnp.dot(latent, up_set[0], preferred_element_type=jnp.float32).astype(jnp.bfloat16)
    key_rows = jnp.dot(latent, up_set[1], preferred_element_type=jnp.float32).astype(jnp.bfloat16)
    values = jnp.dot(latent, up_set[2], preferred_element_type=jnp.float32).astype(jnp.bfloat16)
    query_heads = queries.reshape(tokens, head_count, HEAD_DIM).astype(jnp.float32)
    key_heads = key_rows.reshape(tokens, head_count, HEAD_DIM).astype(jnp.float32)
    value_heads = values.reshape(tokens, head_count, HEAD_DIM).astype(jnp.float32)
    scores = jnp.einsum('qhd,khd->hqk', query_heads, key_heads) / math.sqrt(HEAD_DIM)
    causal = jnp.arange(tokens)[:, None] >= jnp.arange(tokens)[None, :]
    scores = jnp.where(causal[None], scores, -1e+30)
    row_max = lax.optimization_barrier(jnp.max(scores, axis=-1, keepdims=True))
    exponent = jnp.exp(scores - row_max)
    attn_weights = (exponent / lax.optimization_barrier(jnp.sum(exponent, axis=-1, keepdims=True))).astype(jnp.bfloat16)
    mixed_heads = jnp.einsum('hqk,khd->qhd', attn_weights.astype(jnp.float32), value_heads)
    mixed_heads = mixed_heads.astype(jnp.bfloat16).reshape(tokens, head_count * HEAD_DIM)
    merged = lax.dot_general(mixed_heads, down_set[1], contract, preferred_element_type=jnp.float32).astype(jnp.bfloat16)
    branch = jnp.dot(merged, up_set[3], preferred_element_type=jnp.float32)
    return (widened + branch).astype(jnp.bfloat16)

def sequence_loss(final, target_seq, count_total):
    diff_rows = final.astype(jnp.float32) - target_seq.astype(jnp.float32)
    return 0.5 * jnp.sum(diff_rows * diff_rows) / count_total

def reference(hidden_in, targets, down_factors, up_factors, down_dir, up_dir):
    count_total = N_DP * MICRO * TOK

    def total_loss(down_wide, up_wide):

        def one_sequence(carry, pair):
            current = pair[0]
            for section_idx in range(SECTIONS):
                current = layer_step(current, down_wide[section_idx].astype(jnp.bfloat16), up_wide[section_idx].astype(jnp.bfloat16))
            return (carry + sequence_loss(current, pair[1], count_total), None)
        summed, _ = lax.scan(one_sequence, jnp.zeros((), jnp.float32), (hidden_in, targets))
        return summed
    gradient = jax.grad(total_loss, argnums=(0, 1))
    _, curvature = jax.jvp(gradient, (down_factors.astype(jnp.float32), up_factors.astype(jnp.float32)), (down_dir.astype(jnp.float32), up_dir.astype(jnp.float32)))
    return (curvature[0], curvature[1])
```

```python
import functools
import math

import jax
import jax.numpy as jnp
from jax import lax
from jax.experimental import pallas as pl
from jax.experimental.pallas import tpu as pltpu
from jax.sharding import PartitionSpec as P

HEAD_DIM = 128
EPS = 1e-05
BF = jnp.bfloat16
F32 = jnp.float32


def _dot(a, b, dims):
    return lax.dot_general(
        a.astype(BF), b.astype(BF), (dims, ((), ())), preferred_element_type=F32
    )


def nn(a, b):
    return _dot(a, b, ((1,), (0,)))


def nt(a, b):
    return _dot(a, b, ((1,), (1,)))


def tn(a, b):
    return _dot(a, b, ((0,), (0,)))


def rowsum(x):
    return jnp.sum(x, axis=-1, keepdims=True)


def col(x, k, n=1):
    return x[:, k * 128 : (k + n) * 128]


def nt_blocks(x, f_ref, which):
    blocks, cols = f_ref.shape[0], f_ref.shape[3]
    return sum(nt(x[:, b * cols : (b + 1) * cols], f_ref[b, which]) for b in range(blocks))


def nn_blocks(x, f_ref, which):
    return jnp.concatenate([nn(x, f_ref[b, which]) for b in range(f_ref.shape[0])], axis=1)


PF, OF, PT, OT = 0, 1, 2, 3


def project(h, hd, f_ref, fac, tan):
    return nt_blocks(h, f_ref, fac), nt_blocks(hd, f_ref, fac) + nt_blocks(h, f_ref, tan)


def expand(m, md, f_ref, fac, tan):
    return nn_blocks(m, f_ref, fac), nn_blocks(md, f_ref, fac) + nn_blocks(m, f_ref, tan)


def causal_mask(chunk, tokens):
    row = lax.broadcasted_iota(jnp.int32, (chunk, chunk), 0)
    colm = lax.broadcasted_iota(jnp.int32, (chunk, chunk), 1)
    return (row // tokens == colm // tokens) & (colm <= row)


def head_parts(lat, latd, w):
    y = nn(lat, w)
    yd = nn(latd, w[:, :256])
    a, c = y[:, :128], y[:, 128:256]
    ad, cd = y[:, 256:384] + yd[:, :128], y[:, 384:] + yd[:, 128:]
    return a.astype(BF), c.astype(BF), ad.astype(BF), cd.astype(BF)


def weights_of(a, ad, lat, latd, mask):
    s = jnp.where(mask, nt(a, lat), -1e30)
    sd = nt(ad, lat) + nt(a, latd)
    e = jnp.exp(s - jnp.max(s, axis=-1, keepdims=True))
    p = e / rowsum(e)
    pd = p * (sd - rowsum(p * sd))
    return p, pd


def chunk_of(rows, tokens):
    return tokens * 2 if rows % (tokens * 2) == 0 else tokens


def attend(lat, latd, mw_ref, tokens):
    rows = lat.shape[0]
    step = chunk_of(rows, tokens)
    mask = causal_mask(step, tokens)
    out, outd = [], []
    for r in range(0, rows, step):
        la, ld = lat[r : r + step], latd[r : r + step]
        m = md = 0.0
        for k in range(mw_ref.shape[0]):
            a, c, ad, cd = head_parts(la, ld, mw_ref[k])
            p, pd = weights_of(a, ad, la, ld, mask)
            m = m + nn(p, c)
            md = md + nn(pd, c) + nn(p, cd)
        out.append(m)
        outd.append(md)
    return jnp.concatenate(out, axis=0), jnp.concatenate(outd, axis=0)


def attend_back(lat, latd, mu, mud, mw_ref, gmw_ref, tokens):
    rows = lat.shape[0]
    step = chunk_of(rows, tokens)
    mask = causal_mask(step, tokens)
    spans = range(0, rows, step)
    lam = [0.0 for _ in spans]
    lamd = [0.0 for _ in spans]
    for k in range(mw_ref.shape[0]):
        w = mw_ref[k]
        gm = gw = gmd = gwd = 0.0
        for n, r in enumerate(spans):
            la, ld = lat[r : r + step], latd[r : r + step]
            u, ud = mu[r : r + step], mud[r : r + step]
            a, c, ad, cd = head_parts(la, ld, w)
            p, pd = weights_of(a, ad, la, ld, mask)
            pb = nt(u, c)
            pbd = nt(ud, c) + nt(u, cd)
            cb = tn(p, u)
            cbd = tn(pd, u) + tn(p, ud)
            dev = pb - rowsum(p * pb)
            sb = p * dev
            sbd = pd * dev + p * (pbd - rowsum(pd * pb + p * pbd))
            ab = nn(sb, la)
            abd = nn(sbd, la) + nn(sb, ld)
            lam[n] = lam[n] + tn(sb, a) + nt(ab, w[:, :128]) + nt(cb, w[:, 128:256])
            lamd[n] = (
                lamd[n]
                + tn(sbd, a)
                + tn(sb, ad)
                + nt(abd, w[:, :128])
                + nt(ab, w[:, 256:384])
                + nt(cbd, w[:, 128:256])
                + nt(cb, w[:, 384:])
            )
            gm = gm + tn(la, ab)
            gmd = gmd + tn(ld, ab) + tn(la, abd)
            gw = gw + tn(la, cb)
            gwd = gwd + tn(ld, cb) + tn(la, cbd)
        gmw_ref[k] = jnp.concatenate([gm, gw, gmd, gwd], axis=1).astype(BF)
    return jnp.concatenate(lam, axis=0), jnp.concatenate(lamd, axis=0)


def both(a_ref, b_ref):
    return a_ref[...].astype(F32) + b_ref[...].astype(F32)


def lanes(*cols):
    lane = lax.broadcasted_iota(jnp.int32, (cols[0].shape[0], 128), 1)
    out = jnp.zeros(lane.shape, F32)
    for k, c in enumerate(cols):
        out = jnp.where(lane == k, c, out)
    return out


def fold_kernel(scale, down_ref, up_ref, ddir_ref, udir_ref, mw_ref, f_ref):
    for k in range(mw_ref.shape[0]):
        at = slice(k * 128, (k + 1) * 128)
        q, kk, v, p1 = up_ref[0, :, at], up_ref[1, :, at], up_ref[2, :, at], down_ref[1, :, at]
        qd, kd, vd, p1d = (
            udir_ref[0, :, at],
            udir_ref[1, :, at],
            udir_ref[2, :, at],
            ddir_ref[1, :, at],
        )
        mw_ref[k] = jnp.concatenate(
            [
                nt(q, kk) * scale,
                nt(v, p1),
                (nt(qd, kk) + nt(q, kd)) * scale,
                nt(vd, p1) + nt(v, p1d),
            ],
            axis=1,
        ).astype(BF)
    f_ref[PF] = down_ref[0]
    f_ref[OF] = up_ref[3]
    f_ref[PT] = ddir_ref[0]
    f_ref[OT] = udir_ref[3]


def start_kernel(x_ref, f_ref, out_ref):
    x = x_ref[...]
    wide = x.astype(F32)
    a = nt_blocks(x, f_ref, PF)
    ad = nt_blocks(x, f_ref, PT)
    out_ref[...] = jnp.concatenate([a, ad, lanes(rowsum(wide * wide))], axis=1)


def gram_kernel(last, fl_ref, fn_ref, out_ref):
    parts = []
    blocks = range(fl_ref.shape[0])
    if not last:
        g = sum(nt(fl_ref[b, OF], fn_ref[b, PF]) for b in blocks)
        gd = sum(nt(fl_ref[b, OT], fn_ref[b, PF]) + nt(fl_ref[b, OF], fn_ref[b, PT]) for b in blocks)
        parts = [g, gd]
    h = sum(nt(fl_ref[b, OF], fl_ref[b, OF]) for b in blocks)
    hd = sum(nt(fl_ref[b, OT], fl_ref[b, OF]) + nt(fl_ref[b, OF], fl_ref[b, OT]) for b in blocks)
    out_ref[...] = jnp.concatenate([*parts, h, hd], axis=1).astype(BF)


S_PRE, S_PRED, S_R, S_M, S_MD, S_W, S_WD = range(7)


def fwd_kernel(first, last, tokens, width, *refs):
    refs = list(refs)
    ra, rb = refs.pop(0), refs.pop(0)
    got = both(ra, rb)
    if not first:
        ga, gb = refs.pop(0), refs.pop(0)
        gram = both(ga, gb)
        old_ref, fp_ref = refs.pop(0), refs.pop(0)
    h_ref = refs.pop(0)
    if not first:
        hd_ref = refs.pop(0)
    fl_ref = refs.pop(0)
    fn_ref = refs.pop(0)
    mw_ref = refs.pop(0)
    pay_ref, lat_ref, save_ref, ho_ref, hdo_ref = refs

    if first:
        pre, pred = col(got, 0), col(got, 1)
        n = got[:, 256:257]
        nd = jnp.zeros_like(n)
        m = md = w = wd = jnp.zeros_like(pre)
        h = h_ref[...].astype(F32)
        hd = jnp.zeros_like(h)
    else:
        m, md, al, ald, be, bed = (col(got, k) for k in range(6))
        g, gd, hh, hhd = (col(gram, k) for k in range(4))
        pre = al + nn(m, g)
        pred = ald + nn(md, g) + nn(m, gd)
        mh = nn(m, hh)
        mhd = nn(md, hh) + nn(m, hhd)
        w, wd = be + mh, bed + mhd
        old = old_ref[...]
        n = old[:, S_R * 128 + 2 : S_R * 128 + 3] + rowsum(m * (be + w))
        nd = old[:, S_R * 128 + 3 : S_R * 128 + 4] + rowsum(md * (be + w) + m * (bed + wd))
        up, upd = expand(m, md, fp_ref, OF, OT)
        h = h_ref[...] + up
        hd = hd_ref[...] + upd
    r = lax.rsqrt(n / width + EPS)
    rd = -0.5 * r * r * r * (nd / width)
    lat = (r * pre).astype(BF)
    latd = (rd * pre + r * pred).astype(BF)
    lat_ref[...] = jnp.concatenate([lat, latd], axis=1)
    save_ref[...] = jnp.concatenate([pre, pred, lanes(r, rd, n, nd), m, md, w, wd], axis=1)
    ho_ref[...] = h
    hdo_ref[...] = hd
    mo, mod = attend(lat, latd, mw_ref, tokens)
    if last:
        e, ed = project(h - fn_ref[...].astype(F32), hd, fl_ref, OF, OT)
        parts = [mo, mod, e, ed]
    else:
        al, ald = project(h, hd, fn_ref, PF, PT)
        be, bed = project(h, hd, fl_ref, OF, OT)
        parts = [mo, mod, al, ald, be, bed]
    pay_ref[...] = jnp.concatenate(parts, axis=1).astype(BF)


def norm_back(lam, lamd, save, width):
    pre, pred = col(save, S_PRE), col(save, S_PRED)
    r, rd = save[:, S_R * 128 : S_R * 128 + 1], save[:, S_R * 128 + 1 : S_R * 128 + 2]
    pi, pid = r * lam, rd * lam + r * lamd
    sg = rowsum(lam * pre)
    sgd = rowsum(lamd * pre + lam * pred)
    ka = -(r * r * r) * sg / width
    kad = -(3.0 * r * r * rd * sg + r * r * r * sgd) / width
    return pi, pid, ka, kad


def bwd_kernel(first, last, tokens, width, count, *refs):
    refs = list(refs)
    ra, rb, ga, gb = (refs.pop(0) for _ in range(4))
    got, gram = both(ra, rb), both(ga, gb)
    lat_ref, fl_ref, mw_ref = (refs.pop(0) for _ in range(3))
    if first:
        h_ref, hd_ref, y_ref = (refs.pop(0) for _ in range(3))
    else:
        save_ref, fn_ref, h_ref, hd_ref, gi_ref, gdi_ref = (refs.pop(0) for _ in range(6))
    if not last:
        fp_ref = refs.pop(0)
    pay_ref, go_ref, gdo_ref, hvo_ref, gmw_ref = (refs.pop(0) for _ in range(5))
    if first:
        m, md, e, ed = (col(got, k) for k in range(4))
        hh, hhd = col(gram, 0), col(gram, 1)
        mu = (e + nn(m, hh)) / count
        mud = (ed + nn(md, hh) + nn(m, hhd)) / count
        up, upd = expand(m, md, fl_ref, OF, OT)
        g = (h_ref[...] + up - y_ref[...].astype(F32)) / count
        gd = (hd_ref[...] + upd) / count
    else:
        hvp_ref = refs.pop(0)
        lam, lamd, ga0, gad0 = (col(got, k) for k in range(4))
        gg, ggd = col(gram, 0), col(gram, 1)
        save = save_ref[...]
        m, md, w, wd = (col(save, k) for k in (S_M, S_MD, S_W, S_WD))
        pi, pid, ka, kad = norm_back(lam, lamd, save, width)
        mu = ga0 + nt(pi, gg) + ka * w
        mud = gad0 + nt(pid, gg) + nt(pi, ggd) + kad * w + ka * wd
        h, hd = h_ref[...], hd_ref[...]
        up, upd = expand(pi, pid, fn_ref, PF, PT)
        g = gi_ref[...] + up + ka * h
        gd = gdi_ref[...] + upd + kad * h + ka * hd
        hvp_ref[...] = (tn(pid, h) + tn(pi, hd)).astype(BF)
    go_ref[...] = g
    gdo_ref[...] = gd
    hvo_ref[...] = (tn(md, g) + tn(m, gd)).astype(BF)
    lat = lat_ref[...]
    lo, lod = attend_back(
        lat[:, :128], lat[:, 128:], mu.astype(BF), mud.astype(BF), mw_ref, gmw_ref, tokens
    )
    parts = [lo, lod]
    if not last:
        parts.extend(project(g, gd, fp_ref, OF, OT))
    pay_ref[...] = jnp.concatenate(parts, axis=1).astype(BF)


def end_kernel(width, ra_ref, rb_ref, save_ref, h_ref, hd_ref, hvp_ref):
    got = both(ra_ref, rb_ref)
    pi, pid, _, _ = norm_back(col(got, 0), col(got, 1), save_ref[...], width)
    hvp_ref[...] = (tn(pid, h_ref[...]) + tn(pi, hd_ref[...])).astype(BF)


def unfold_kernel(scale, gmw_ref, hvp_ref, hvo_ref, down_ref, up_ref, ddir_ref, udir_ref, od_ref, ou_ref):
    od_ref[0] = hvp_ref[...].astype(F32)
    ou_ref[3] = hvo_ref[...].astype(F32)
    for k in range(gmw_ref.shape[0]):
        at = slice(k * 128, (k + 1) * 128)
        w = gmw_ref[k]
        gm, gw, gmd, gwd = (w[:, n * 128 : (n + 1) * 128] for n in range(4))
        q, kk, v, p1 = up_ref[0, :, at], up_ref[1, :, at], up_ref[2, :, at], down_ref[1, :, at]
        qd, kd, vd, p1d = (
            udir_ref[0, :, at],
            udir_ref[1, :, at],
            udir_ref[2, :, at],
            ddir_ref[1, :, at],
        )
        ou_ref[0, :, at] = (nn(gmd, kk) + nn(gm, kd)) * scale
        ou_ref[1, :, at] = (tn(gmd, q) + tn(gm, qd)) * scale
        ou_ref[2, :, at] = nn(gwd, p1) + nn(gw, p1d)
        od_ref[1, :, at] = tn(gwd, v) + tn(gw, vd)


def call(kernel, outs, *args, flops=2e9):
    size = sum(a.size * a.dtype.itemsize for a in args)
    return pl.pallas_call(
        kernel,
        out_shape=[jax.ShapeDtypeStruct(shape, kind) for shape, kind in outs],
        in_specs=[pl.BlockSpec(memory_space=pltpu.VMEM)] * len(args),
        out_specs=[pl.BlockSpec(memory_space=pltpu.VMEM)] * len(outs),
        compiler_params=pltpu.CompilerParams(vmem_limit_bytes=48 * 1024 * 1024),
        cost_estimate=pl.CostEstimate(
            flops=int(flops), bytes_accessed=int(size), transcendentals=0
        ),
    )(*args)


def body(hidden_in, targets, down_factors, up_factors, down_dir, up_dir):
    dp, sections = lax.axis_size("dp"), lax.axis_size("section")
    micro, tokens, width = hidden_in.shape
    rank, cols = down_factors.shape[2], down_factors.shape[3]
    fan = 2 if dp % 2 == 0 and (dp // 2) % sections == 0 else 1
    team = dp // fan
    per = team // sections
    heads = cols // HEAD_DIM
    rows = per * micro * tokens
    wide = fan * cols
    count = micro * tokens * dp
    scale = 1.0 / math.sqrt(HEAD_DIM)
    i, s = lax.axis_index("dp"), lax.axis_index("section")
    j, gi = i % team, i // team
    flat = lambda a, b: a * sections + b

    def over_dp(x, bit, only=None):
        if only is None:
            return lax.ppermute(x, "dp", [(a, a ^ bit) for a in range(dp)])
        pairs = [(flat(a, b), flat(a ^ bit, b)) for a in range(dp) for b in only]
        return lax.ppermute(x, ("dp", "section"), pairs)

    def reduce_pair(x):
        bit = 1
        while bit * 2 < team:
            x = (x.astype(F32) + over_dp(x, bit).astype(F32)).astype(x.dtype)
            bit *= 2
        return x, over_dp(x, bit)

    def share(x, to):
        v = x.reshape(micro, tokens, fan, team, cols)
        v = lax.dynamic_index_in_dim(v, to, 3, keepdims=False)
        v = jnp.concatenate(
            [lax.dynamic_index_in_dim(v, gi ^ b, 2, keepdims=False) for b in range(fan)], axis=-1
        )
        return v.reshape(micro * tokens, wide)

    def pair_share(to):
        return jnp.stack([share(hidden_in, to), share(targets, to)])

    slots = [jnp.zeros((2, micro * tokens, wide), BF) for _ in range(per)]
    for step in range(team):
        mine = pair_share(j ^ step)
        if step == 0:
            got = jnp.where(j // per == s, mine, jnp.zeros_like(mine))
        else:
            pairs = [
                (flat(b * team + a, c), flat(b * team + (a ^ step), c))
                for b in range(fan)
                for a in range(team)
                for c in range(sections)
                if a // per == c
            ]
            got = lax.ppermute(mine, ("dp", "section"), pairs)
        here = (j ^ step) % per
        for q in range(per):
            slots[q] = slots[q] + (got if per == 1 else jnp.where(here == q, got, jnp.zeros_like(got)))
    xy = slots[0] if per == 1 else jnp.concatenate(slots, axis=1)
    x_loc, y_loc = xy[0], xy[1]

    own = (down_factors[0], up_factors[0], down_dir[0], up_dir[0])
    mw_own, f_own = call(
        functools.partial(fold_kernel, scale),
        [((heads, rank, 4 * rank), BF), ((4, rank, cols), BF)],
        *own,
    )

    def gathered(x, only):
        return jnp.stack([x, over_dp(x, team, only)]) if fan == 2 else x[None]

    def spread(x, layer):
        far = layer ^ 2
        a = lax.ppermute(x, "section", [(layer, far)])
        v = jnp.where(s == layer, x, a)
        b = lax.ppermute(v, "section", [(layer, layer ^ 1), (far, far ^ 1)])
        return jnp.where((s == layer) | (s == far), v, b)

    facs, mws = [], []
    for layer in range(sections):
        f = spread(gathered(f_own, [layer]), layer)
        w = spread(gathered(mw_own, [layer]), layer)
        facs.append(f)
        mws.append(w.reshape(fan * heads, rank, 4 * rank))

    (a0,) = call(start_kernel, [((rows, 3 * rank), F32)], x_loc, facs[0])
    state = reduce_pair(a0)
    grams = []
    for layer in range(sections):
        last = layer == sections - 1
        (gp,) = call(
            functools.partial(gram_kernel, last),
            [((rank, (2 if last else 4) * rank), BF)],
            facs[layer],
            facs[layer if last else layer + 1],
        )
        grams.append(reduce_pair(gp))

    lats, saves, hs = [], [], []
    for layer in range(sections):
        first, last = layer == 0, layer == sections - 1
        args = [*state]
        if first:
            args += [x_loc]
        else:
            args += [*grams[layer - 1], saves[-1], facs[layer - 1], *hs[-1]]
        args += [facs[layer], y_loc if last else facs[layer + 1], mws[layer]]
        pay, lat, save, h, hd = call(
            functools.partial(fwd_kernel, first, last, tokens, width),
            [
                ((rows, (4 if last else 6) * rank), BF),
                ((rows, 2 * rank), BF),
                ((rows, 7 * rank), F32),
                ((rows, wide), F32),
                ((rows, wide), F32),
            ],
            *args,
        )
        lats.append(lat)
        saves.append(save)
        hs.append((h, hd))
        state = reduce_pair(pay)

    def collect(x, layer, axis):
        far = layer ^ 2
        v = x + lax.ppermute(x, "section", [(layer ^ 1, layer), (far ^ 1, far)])
        v = v + lax.ppermute(v, "section", [(far, layer)])
        if fan == 1:
            return v
        half = x.shape[axis] // 2
        keep = lax.slice_in_dim(v, 0, half, axis=axis)
        give = lax.slice_in_dim(v, half, 2 * half, axis=axis)
        return keep + over_dp(give, team, [layer])

    hv_p, hv_o, gmws = [None] * sections, [None] * sections, [None] * sections
    gcur = None
    for layer in reversed(range(sections)):
        first, last = layer == sections - 1, layer == 0
        args = [*state, *grams[layer], lats[layer], facs[layer], mws[layer]]
        if first:
            args += [*hs[layer], y_loc]
        else:
            args += [saves[layer + 1], facs[layer + 1], *hs[layer + 1], *gcur]
        if not last:
            args += [facs[layer - 1]]
        outs = [
            ((rows, (2 if last else 4) * rank), BF),
            ((rows, wide), F32),
            ((rows, wide), F32),
            ((rank, wide), BF),
            ((fan * heads, rank, 4 * rank), BF),
        ]
        if not first:
            outs += [((rank, wide), BF)]
        res = call(
            functools.partial(bwd_kernel, first, last, tokens, width, float(count)), outs, *args
        )
        pay, gcur = res[0], (res[1], res[2])
        state = reduce_pair(pay)
        hv_o[layer] = collect(res[3], layer, 1)
        gmws[layer] = collect(res[4], layer, 0)
        if not first:
            hv_p[layer + 1] = collect(res[5], layer + 1, 1)
    (hvp0,) = call(
        functools.partial(end_kernel, width),
        [((rank, wide), BF)],
        *state,
        saves[0],
        *hs[0],
    )
    hv_p[0] = collect(hvp0, 0, 1)

    def pick(parts):
        out = parts[0]
        for layer in range(1, sections):
            out = jnp.where(s == layer, parts[layer], out)
        return out

    part_down, part_up = call(
        functools.partial(unfold_kernel, scale),
        [((2, rank, cols), F32), ((4, rank, cols), F32)],
        pick(gmws),
        pick(hv_p),
        pick(hv_o),
        *own,
    )
    return (part_down[None], part_up[None])


def solution(mesh):
    in_specs = (
        P("dp", None, None),
        P("dp", None, None),
        P("section", None, None, "dp"),
        P("section", None, None, "dp"),
        P("section", None, None, "dp"),
        P("section", None, None, "dp"),
    )
    out_specs = (P("section", None, None, "dp"), P("section", None, None, "dp"))
    return jax.shard_map(body, mesh=mesh, in_specs=in_specs, out_specs=out_specs, check_vma=False)
```

```python
import functools
import math

import jax
import jax.numpy as jnp
from jax import lax
from jax.experimental import pallas as pl
from jax.experimental.pallas import tpu as pltpu
from jax.sharding import PartitionSpec as P

HEAD_DIM = 128
EPS = 1e-05
BF = jnp.bfloat16
F32 = jnp.float32


def _dot(a, b, dims):
    return lax.dot_general(
        a.astype(BF), b.astype(BF), (dims, ((), ())), preferred_element_type=F32
    )


def nn(a, b):
    return _dot(a, b, ((1,), (0,)))


def nt(a, b):
    return _dot(a, b, ((1,), (1,)))


def tn(a, b):
    return _dot(a, b, ((0,), (0,)))


def rowsum(x):
    return jnp.sum(x, axis=-1, keepdims=True)


def col(x, k, n=1):
    return x[:, k * 128 : (k + n) * 128]


def nt_blocks(x, f_ref, which):
    blocks, cols = f_ref.shape[0], f_ref.shape[3]
    return sum(nt(x[:, b * cols : (b + 1) * cols], f_ref[b, which]) for b in range(blocks))


def nn_blocks(x, f_ref, which):
    return jnp.concatenate([nn(x, f_ref[b, which]) for b in range(f_ref.shape[0])], axis=1)


PF, OF, PT, OT = 0, 1, 2, 3


def project(h, hd, f_ref, fac, tan):
    return nt_blocks(h, f_ref, fac), nt_blocks(hd, f_ref, fac) + nt_blocks(h, f_ref, tan)


def expand(m, md, f_ref, fac, tan):
    return nn_blocks(m, f_ref, fac), nn_blocks(md, f_ref, fac) + nn_blocks(m, f_ref, tan)


def causal_mask(chunk, tokens):
    row = lax.broadcasted_iota(jnp.int32, (chunk, chunk), 0)
    colm = lax.broadcasted_iota(jnp.int32, (chunk, chunk), 1)
    return (row // tokens == colm // tokens) & (colm <= row)


def chunk_of(rows, tokens):
    return tokens * 2 if rows % (tokens * 2) == 0 else tokens


def cat(*parts, axis=1):
    return jnp.concatenate(parts, axis=axis)


def head_parts(lat, both_lat, w):
    y = nn(lat, w[:128]).astype(BF)
    yd = nn(both_lat, w).astype(BF)
    return y[:, :128], y[:, 128:], yd[:, :128], yd[:, 128:]


def weights_of(a, ad, lat, lat_pair, mask):
    s = jnp.where(mask, nt(a, lat), -1e30)
    sd = nt(cat(ad, a), lat_pair)
    e = jnp.exp(s - jnp.max(s, axis=-1, keepdims=True))
    p = e * (1.0 / rowsum(e))
    pd = p * (sd - rowsum(p * sd))
    return p, pd


def attend(lat, latd, mw_ref, tokens):
    rows = lat.shape[0]
    step = chunk_of(rows, tokens)
    mask = causal_mask(step, tokens)
    out, outd = [], []
    for r in range(0, rows, step):
        la, ld = lat[r : r + step], latd[r : r + step]
        pair, flip = cat(la, ld), cat(ld, la)
        m = md = 0.0
        for k in range(mw_ref.shape[0]):
            a, c, ad, cd = head_parts(la, flip, mw_ref[k])
            p, pd = weights_of(a, ad, la, pair, mask)
            m = m + nn(p, c)
            md = md + nn(cat(pd.astype(BF), p.astype(BF)), cat(c, cd, axis=0))
        out.append(m)
        outd.append(md)
    return cat(*out, axis=0), cat(*outd, axis=0)


def attend_back(lat, latd, mu, mud, mw_ref, store, tokens):
    rows = lat.shape[0]
    step = chunk_of(rows, tokens)
    mask = causal_mask(step, tokens)
    spans = range(0, rows, step)
    lam = [0.0 for _ in spans]
    lamd = [0.0 for _ in spans]
    for k in range(mw_ref.shape[0]):
        w = mw_ref[k]
        g = gd = 0.0
        for n, r in enumerate(spans):
            la, ld = lat[r : r + step], latd[r : r + step]
            u, ud = mu[r : r + step], mud[r : r + step]
            pair, flip = cat(la, ld), cat(ld, la)
            a, c, ad, cd = head_parts(la, flip, w)
            p, pd = weights_of(a, ad, la, pair, mask)
            pb = nt(u, c)
            pbd = nt(cat(ud, u), cat(c, cd))
            pl_, pdl = p.astype(BF), pd.astype(BF)
            cb = tn(pl_, u)
            cbd = tn(cat(pdl, pl_, axis=0), cat(u, ud, axis=0))
            dev = pb - rowsum(p * pb)
            sb = p * dev
            sbd = pd * dev + p * (pbd - rowsum(pd * pb + p * pbd))
            sbl, sbdl = sb.astype(BF), sbd.astype(BF)
            ab = nn(sbl, la)
            abd = nn(cat(sbdl, sbl), cat(la, ld, axis=0))
            back = cat(ab, cb).astype(BF)
            backd = cat(abd, cbd).astype(BF)
            lam[n] = lam[n] + tn(sbl, a) + nt(back, w[:128])
            lamd[n] = (
                lamd[n]
                + tn(cat(sbdl, sbl, axis=0), cat(a, ad, axis=0))
                + nt(backd, w[:128])
                + nt(back, w[128:])
            )
            g = g + tn(la, back)
            gd = gd + tn(cat(ld, la, axis=0), cat(back, backd, axis=0))
        store(k, g, gd)
    return cat(*lam, axis=0), cat(*lamd, axis=0)


def both(a_ref, b_ref):
    return a_ref[...].astype(F32) + b_ref[...].astype(F32)


def lanes(*cols):
    lane = lax.broadcasted_iota(jnp.int32, (cols[0].shape[0], 128), 1)
    out = jnp.zeros(lane.shape, F32)
    for k, c in enumerate(cols):
        out = jnp.where(lane == k, c, out)
    return out


def fold_kernel(scale, down_any, up_any, ddir_any, udir_any, mw_ref, f_ref, down, up, ddir, udir, sems):
    copies = [
        pltpu.make_async_copy(src, dst, sems.at[n])
        for n, (src, dst) in enumerate(
            [(down_any, down), (up_any, up), (ddir_any, ddir), (udir_any, udir)]
        )
    ]
    for c in copies:
        c.start()
    for c in copies:
        c.wait()
    f_ref[PF] = down[0]
    f_ref[OF] = up[3]
    f_ref[PT] = ddir[0]
    f_ref[OT] = udir[3]
    for k in range(mw_ref.shape[0]):
        at = slice(k * 128, (k + 1) * 128)
        q, kk, v, p1 = up[0, :, at], up[1, :, at], up[2, :, at], down[1, :, at]
        qd, kd, vd, p1d = udir[0, :, at], udir[1, :, at], udir[2, :, at], ddir[1, :, at]
        top = cat(nt(q, kk) * scale, nt(v, p1))
        bottom = cat(nt(cat(qd, q), cat(kk, kd)) * scale, nt(cat(vd, v), cat(p1, p1d)))
        mw_ref[k] = cat(top, bottom, axis=0).astype(BF)


def share_kernel(blocks, cols, where_ref, x_any, y_any, out_ref, sems):
    rows = x_any.shape[0]
    copies = []
    for n, src in enumerate((x_any, y_any)):
        for b in range(blocks):
            at = pl.ds(pl.multiple_of(where_ref[b] * cols, cols), cols)
            copies.append(
                pltpu.make_async_copy(
                    src.at[:, at], out_ref.at[n, :, pl.ds(b * cols, cols)], sems.at[n * blocks + b]
                )
            )
    for c in copies:
        c.start()
    for c in copies:
        c.wait()


def assemble_kernel(layers, blocks, s_ref, *refs):
    pieces, outs, sems = refs[: layers * blocks], refs[layers * blocks : -1], refs[-1]
    for slot in range(layers):
        for layer in range(layers):

            @pl.when((s_ref[0] ^ slot) == layer)
            def _():
                for b in range(blocks):
                    pltpu.make_async_copy(
                        pieces[slot * blocks + b], outs[layer].at[b], sems.at[slot * blocks + b]
                    ).start()

    for slot in range(layers):
        for b in range(blocks):
            pltpu.make_async_copy(
                pieces[slot * blocks + b], outs[0].at[b], sems.at[slot * blocks + b]
            ).wait()


def start_kernel(x_ref, f_ref, out_ref):
    x = x_ref[...]
    wide = x.astype(F32)
    a = nt_blocks(x, f_ref, PF)
    ad = nt_blocks(x, f_ref, PT)
    out_ref[...] = jnp.concatenate([a, ad, lanes(rowsum(wide * wide))], axis=1)


def gram_kernel(*refs):
    out_ref, facs = refs[-1], refs[:-1]
    parts = []
    for n, fl in enumerate(facs):
        g = gd = h = hd = 0.0
        for b in range(fl.shape[0]):
            o, ot = fl[b, OF], fl[b, OT]
            if n + 1 < len(facs):
                fn = facs[n + 1]
                g = g + nt(o, fn[b, PF])
                gd = gd + nt(cat(ot, o), cat(fn[b, PF], fn[b, PT]))
            h = h + nt(o, o)
            hd = hd + nt(cat(ot, o), cat(o, ot))
        parts.extend([g, gd, h, hd] if n + 1 < len(facs) else [h, hd])
    out_ref[...] = cat(*parts).astype(BF)


S_PRE, S_PRED, S_R, S_M, S_MD, S_W, S_WD = range(7)


def fwd_kernel(layer, first, last, tokens, width, *refs):
    refs = list(refs)
    ra, rb = refs.pop(0), refs.pop(0)
    got = both(ra, rb)
    if not first:
        ga, gb = refs.pop(0), refs.pop(0)
        at = slice((layer - 1) * 512, layer * 512)
        gram = ga[:, at].astype(F32) + gb[:, at].astype(F32)
        old_ref, fp_ref = refs.pop(0), refs.pop(0)
    h_ref = refs.pop(0)
    if not first:
        hd_ref = refs.pop(0)
    fl_ref = refs.pop(0)
    fn_ref = refs.pop(0)
    mw_ref = refs.pop(0)
    pay_ref, lat_ref, save_ref, ho_ref, hdo_ref = refs

    if first:
        pre, pred = col(got, 0), col(got, 1)
        n = got[:, 256:257]
        nd = jnp.zeros_like(n)
        m = md = w = wd = jnp.zeros_like(pre)
        h = h_ref[...].astype(F32)
        hd = jnp.zeros_like(h)
    else:
        m, md, al, ald, be, bed = (col(got, k) for k in range(6))
        g, gd, hh, hhd = (col(gram, k) for k in range(4))
        pre = al + nn(m, g)
        pred = ald + nn(md, g) + nn(m, gd)
        mh = nn(m, hh)
        mhd = nn(md, hh) + nn(m, hhd)
        w, wd = be + mh, bed + mhd
        old = old_ref[...]
        n = old[:, S_R * 128 + 2 : S_R * 128 + 3] + rowsum(m * (be + w))
        nd = old[:, S_R * 128 + 3 : S_R * 128 + 4] + rowsum(md * (be + w) + m * (bed + wd))
        up, upd = expand(m, md, fp_ref, OF, OT)
        h = h_ref[...] + up
        hd = hd_ref[...] + upd
    r = lax.rsqrt(n / width + EPS)
    rd = -0.5 * r * r * r * (nd / width)
    lat = (r * pre).astype(BF)
    latd = (rd * pre + r * pred).astype(BF)
    lat_ref[...] = jnp.concatenate([lat, latd], axis=1)
    save_ref[...] = jnp.concatenate([pre, pred, lanes(r, rd, n, nd), m, md, w, wd], axis=1)
    ho_ref[...] = h
    hdo_ref[...] = hd
    mo, mod = attend(lat, latd, mw_ref, tokens)
    if last:
        e, ed = project(h - fn_ref[...].astype(F32), hd, fl_ref, OF, OT)
        parts = [mo, mod, e, ed]
    else:
        al, ald = project(h, hd, fn_ref, PF, PT)
        be, bed = project(h, hd, fl_ref, OF, OT)
        parts = [mo, mod, al, ald, be, bed]
    pay_ref[...] = jnp.concatenate(parts, axis=1).astype(BF)


def norm_back(lam, lamd, save, width):
    pre, pred = col(save, S_PRE), col(save, S_PRED)
    r, rd = save[:, S_R * 128 : S_R * 128 + 1], save[:, S_R * 128 + 1 : S_R * 128 + 2]
    pi, pid = r * lam, rd * lam + r * lamd
    sg = rowsum(lam * pre)
    sgd = rowsum(lamd * pre + lam * pred)
    ka = -(r * r * r) * sg / width
    kad = -(3.0 * r * r * rd * sg + r * r * r * sgd) / width
    return pi, pid, ka, kad


def put(keep0, keep1, give, c, at, low, high):
    per = keep0.shape[0]
    k, g = jnp.where(c == 0, low, high).astype(BF), jnp.where(c == 0, high, low).astype(BF)
    if at < per:
        keep0[at] = k
    else:
        keep1[at - per] = k
    give[at] = g


def put_rows(keep0, keep1, give, c, hvo, hvp):
    rank = hvo.shape[0]
    per, pieces = keep0.shape[0], hvo.shape[1] // 128
    blocks = give.shape[0] // per
    base = per - pieces // blocks
    for n in range(pieces):
        b, e = divmod(n, pieces // blocks)
        at = slice(n * 128, (n + 1) * 128)
        low = cat(hvo[: rank // 2, at], hvp[: rank // 2, at], axis=0)
        high = cat(hvo[rank // 2 :, at], hvp[rank // 2 :, at], axis=0)
        put(keep0, keep1, give, c, b * per + base + e, low, high)


def bwd_kernel(layer, first, last, tokens, width, count, deps, *refs):
    refs = list(refs)
    s_ref = refs.pop(0)
    c = s_ref[0] & 1
    ra, rb, ga, gb = (refs.pop(0) for _ in range(4))
    at = slice(layer * 512, layer * 512 + 256)
    got, gram = both(ra, rb), ga[:, at].astype(F32) + gb[:, at].astype(F32)
    lat_ref, fl_ref, mw_ref = (refs.pop(0) for _ in range(3))
    if first:
        h_ref, hd_ref, y_ref = (refs.pop(0) for _ in range(3))
    else:
        save_ref, fn_ref, h_ref, hd_ref, gi_ref, gdi_ref = (refs.pop(0) for _ in range(6))
    if not last:
        fp_ref = refs.pop(0)
    del refs[:deps]
    pay_ref, go_ref, gdo_ref, keep0, keep1, give = refs
    if first:
        m, md, e, ed = (col(got, k) for k in range(4))
        hh, hhd = col(gram, 0), col(gram, 1)
        mu = (e + nn(m, hh)) / count
        mud = (ed + nn(md, hh) + nn(m, hhd)) / count
        up, upd = expand(m, md, fl_ref, OF, OT)
        g = (h_ref[...] + up - y_ref[...].astype(F32)) / count
        gd = (hd_ref[...] + upd) / count
        hvp = jnp.zeros((m.shape[1], g.shape[1]), F32)
    else:
        lam, lamd, ga0, gad0 = (col(got, k) for k in range(4))
        gg, ggd = col(gram, 0), col(gram, 1)
        save = save_ref[...]
        m, md, w, wd = (col(save, k) for k in (S_M, S_MD, S_W, S_WD))
        pi, pid, ka, kad = norm_back(lam, lamd, save, width)
        mu = ga0 + nt(pi, gg) + ka * w
        mud = gad0 + nt(pid, gg) + nt(pi, ggd) + kad * w + ka * wd
        h, hd = h_ref[...], hd_ref[...]
        up, upd = expand(pi, pid, fn_ref, PF, PT)
        g = gi_ref[...] + up + ka * h
        gd = gdi_ref[...] + upd + kad * h + ka * hd
        hvp = tn(pid, h) + tn(pi, hd)
    go_ref[...] = g
    gdo_ref[...] = gd
    put_rows(keep0, keep1, give, c, tn(md, g) + tn(m, gd), hvp)
    lat = lat_ref[...]
    heads = mw_ref.shape[0]
    blocks = give.shape[0] // keep0.shape[0]

    def store(k, gv, gvd):
        b, e = divmod(k, heads // blocks)
        for n in range(2):
            part = slice(n * 128, (n + 1) * 128)
            put(keep0, keep1, give, c, b * keep0.shape[0] + 2 * e + n, gv[:, part], gvd[:, part])

    lo, lod = attend_back(
        lat[:, :128], lat[:, 128:], mu.astype(BF), mud.astype(BF), mw_ref, store, tokens
    )
    parts = [lo, lod]
    if not last:
        parts.extend(project(g, gd, fp_ref, OF, OT))
    pay_ref[...] = cat(*parts).astype(BF)


def end_kernel(width, deps, s_ref, ra_ref, rb_ref, save_ref, h_ref, hd_ref, *refs):
    keep0, keep1, give = refs[deps:]
    got = both(ra_ref, rb_ref)
    pi, pid, _, _ = norm_back(col(got, 0), col(got, 1), save_ref[...], width)
    hvp = tn(pid, h_ref[...]) + tn(pi, hd_ref[...])
    put_rows(keep0, keep1, give, s_ref[0] & 1, jnp.zeros_like(hvp), hvp)


def unfold_kernel(scale, layers, s_ref, *refs):
    refs = list(refs)
    ys, qs = [refs.pop(0) for _ in range(layers)], [refs.pop(0) for _ in range(layers)]
    y0, q0 = refs.pop(0), refs.pop(0)
    down, up, ddir, udir, od_ref, ou_ref, gy, gq, py, pq, sems = refs
    s, heads = s_ref[0], y0.shape[0]
    for layer in range(layers):

        @pl.when(s == layer)
        def _():
            pltpu.make_async_copy(ys[layer], gy, sems.at[0]).start()
            pltpu.make_async_copy(qs[layer], gq, sems.at[1]).start()
            tail = pl.ds(2 * heads, heads)
            py_src = y0 if layer == 0 else ys[layer - 1].at[tail]
            pq_src = q0 if layer == 0 else qs[layer - 1].at[tail]
            pltpu.make_async_copy(py_src, py, sems.at[2]).start()
            pltpu.make_async_copy(pq_src, pq, sems.at[3]).start()

    pltpu.make_async_copy(ys[0], gy, sems.at[0]).wait()
    pltpu.make_async_copy(qs[0], gq, sems.at[1]).wait()
    pltpu.make_async_copy(y0, py, sems.at[2]).wait()
    pltpu.make_async_copy(q0, pq, sems.at[3]).wait()
    even = (s & 1) == 0

    def halves(a, b):
        return jnp.where(even, a, b), jnp.where(even, b, a)

    for k in range(heads):
        at = slice(k * 128, (k + 1) * 128)
        gm, gmd = halves(gy[2 * k], gq[2 * k])
        gw, gwd = halves(gy[2 * k + 1], gq[2 * k + 1])
        top, bottom = halves(gy[2 * heads + k], gq[2 * heads + k])
        half = top.shape[0] // 2
        ou_ref[3, :, at] = cat(top[:half], bottom[:half], axis=0).astype(F32)
        top, bottom = halves(py[k], pq[k])
        od_ref[0, :, at] = cat(top[half:], bottom[half:], axis=0).astype(F32)
        q, kk, v, p1 = up[0, :, at], up[1, :, at], up[2, :, at], down[1, :, at]
        qd, kd, vd, p1d = udir[0, :, at], udir[1, :, at], udir[2, :, at], ddir[1, :, at]
        ou_ref[0, :, at] = nn(cat(gmd, gm), cat(kk, kd, axis=0)) * scale
        ou_ref[1, :, at] = tn(cat(gmd, gm, axis=0), cat(q, qd, axis=0)) * scale
        ou_ref[2, :, at] = nn(cat(gwd, gw), cat(p1, p1d, axis=0))
        od_ref[1, :, at] = tn(cat(gwd, gw, axis=0), cat(v, vd, axis=0))


VM = pl.BlockSpec(memory_space=pltpu.VMEM)
HB = pl.BlockSpec(memory_space=pl.ANY)
SM = pl.BlockSpec(memory_space=pltpu.SMEM)


def call(kernel, outs, *args, specs=None, scratch=(), flops=1e9, limit=24):
    specs = specs or "v" * len(args)
    size = sum(a.size * a.dtype.itemsize for a in args)
    return pl.pallas_call(
        kernel,
        out_shape=[jax.ShapeDtypeStruct(shape, kind) for shape, kind in outs],
        in_specs=[{"v": VM, "a": HB, "s": SM}[c] for c in specs],
        out_specs=[VM] * len(outs),
        scratch_shapes=list(scratch),
        compiler_params=pltpu.CompilerParams(vmem_limit_bytes=limit * 1024 * 1024),
        cost_estimate=pl.CostEstimate(
            flops=int(flops), bytes_accessed=int(size), transcendentals=0
        ),
    )(*args)


def body(hidden_in, targets, down_factors, up_factors, down_dir, up_dir):
    dp, sections = lax.axis_size("dp"), lax.axis_size("section")
    micro, tokens, width = hidden_in.shape
    rank, cols = down_factors.shape[2], down_factors.shape[3]
    fan = 2 if dp % 2 == 0 and (dp // 2) % sections == 0 else 1
    team = dp // fan
    per = team // sections
    heads = cols // HEAD_DIM
    rows = per * micro * tokens
    wide = fan * cols
    count = float(micro * tokens * dp)
    scale = 1.0 / math.sqrt(HEAD_DIM)
    i, s = lax.axis_index("dp"), lax.axis_index("section")
    j, gi = i % team, i // team
    here = jnp.reshape(s, (1,)).astype(jnp.int32)
    dma = pltpu.SemaphoreType.DMA

    def over_dp(x, bit):
        return lax.ppermute(x, "dp", [(a, a ^ bit) for a in range(dp)])

    def over_sec(x, bit):
        return lax.ppermute(x, "section", [(a, a ^ bit) for a in range(sections)])

    def plus(a, b):
        return (a.astype(F32) + b.astype(F32)).astype(a.dtype)

    def reduce_pair(x):
        bit = 1
        while bit * 2 < team:
            x = plus(x, over_dp(x, bit))
            bit *= 2
        return x, over_dp(x, bit)

    def swap(to, turn):
        blocks = jnp.stack([(gi ^ b) * team + to for b in range(fan)]).astype(jnp.int32)
        (mine,) = call(
            functools.partial(share_kernel, fan, cols),
            [((2, micro * tokens, wide), BF)],
            blocks,
            hidden_in.reshape(micro * tokens, width),
            targets.reshape(micro * tokens, width),
            specs="saa",
            scratch=[dma((2 * fan,))],
        )
        pairs = []
        for b in range(fan):
            for a in range(team):
                for c in range(sections):
                    dest = c * per + (a % per + turn) % per
                    pairs.append(
                        ((b * team + a) * sections + c, (b * team + dest) * sections + a // per)
                    )
        return lax.ppermute(mine, ("dp", "section"), pairs)

    if per == 1:
        xy = swap(s, 0)
    else:
        slots = [jnp.zeros((2, micro * tokens, wide), BF) for _ in range(per)]
        for turn in range(per):
            got = swap(s * per + (j + turn) % per, turn)
            at = (j - turn) % per
            for q in range(per):
                slots[q] = slots[q] + jnp.where(at == q, got, jnp.zeros_like(got))
        xy = jnp.concatenate(slots, axis=1)
    x_loc, y_loc = xy[0], xy[1]

    own = (down_factors[0], up_factors[0], down_dir[0], up_dir[0])
    mw_own, f_own = call(
        functools.partial(fold_kernel, scale),
        [((heads, 2 * rank, 2 * rank), BF), ((4, rank, cols), BF)],
        *own,
        specs="aaaa",
        scratch=[pltpu.VMEM(a.shape, a.dtype) for a in own] + [dma((4,))],
    )

    def everywhere(x):
        slots = [[x] + ([over_dp(x, team)] if fan == 2 else [])]
        bit = sections // 2
        steps = [0]
        while bit:
            slots += [[over_sec(v, bit) for v in parts] for parts in slots]
            steps += [k ^ bit for k in steps]
            bit //= 2
        flat = [v for k in range(sections) for v in slots[steps.index(k)]]
        return call(
            functools.partial(assemble_kernel, sections, fan),
            [((fan, *x.shape), BF)] * sections,
            here,
            *flat,
            specs="s" + "a" * len(flat),
            scratch=[dma((len(flat),))],
            flops=1e6,
        )

    facs = everywhere(f_own)
    mws = [w.reshape(fan * heads, 2 * rank, 2 * rank) for w in everywhere(mw_own)]

    (a0,) = call(start_kernel, [((rows, 3 * rank), F32)], x_loc, facs[0])
    state = reduce_pair(a0)
    (gp,) = call(gram_kernel, [((rank, (4 * sections - 2) * rank), BF)], *facs)
    grams = reduce_pair(gp)

    lats, saves, hs = [], [], []
    for layer in range(sections):
        first, last = layer == 0, layer == sections - 1
        args = [*state]
        if first:
            args += [x_loc]
        else:
            args += [*grams, saves[-1], facs[layer - 1], *hs[-1]]
        args += [facs[layer], y_loc if last else facs[layer + 1], mws[layer]]
        pay, lat, save, h, hd = call(
            functools.partial(fwd_kernel, layer, first, last, tokens, width),
            [
                ((rows, (4 if last else 6) * rank), BF),
                ((rows, 2 * rank), BF),
                ((rows, 7 * rank), F32),
                ((rows, wide), F32),
                ((rows, wide), F32),
            ],
            *args,
        )
        lats.append(lat)
        saves.append(save)
        hs.append((h, hd))
        state = reduce_pair(pay)

    def hop_core(keep0, keep1, give):
        got = over_sec(give, 1)
        n = keep0.shape[0]
        return plus(keep0, got[:n]), (plus(keep1, got[n:]) if fan == 2 else None)

    def hop_dp(v0, v1):
        return plus(v0, over_dp(v1, team)) if fan == 2 else v0

    def hop_far(w):
        bit = 2
        while bit < sections:
            w = plus(w, over_sec(w, bit))
            bit *= 2
        return w

    bundle = 3 * heads
    stage1, stage2, stage3 = {}, {}, {}
    gcur = None
    for layer in reversed(range(sections)):
        first, last = layer == sections - 1, layer == 0
        if layer + 3 in stage2:
            stage3[layer + 3] = hop_far(stage2[layer + 3])
        if layer + 2 in stage1:
            stage2[layer + 2] = hop_dp(*stage1[layer + 2])
        deps = []
        if layer + 1 in stage1:
            deps += [v for v in stage1[layer + 1] if v is not None]
        if layer + 2 in stage2:
            deps += [stage2[layer + 2]]
        if layer + 3 in stage3:
            deps += [stage3[layer + 3]]
        args = [here, *state, *grams, lats[layer], facs[layer], mws[layer]]
        if first:
            args += [*hs[layer], y_loc]
        else:
            args += [saves[layer + 1], facs[layer + 1], *hs[layer + 1], *gcur]
        if not last:
            args += [facs[layer - 1]]
        specs = "s" + "v" * (len(args) - 1) + "a" * len(deps)
        pay, g, gd, *made = call(
            functools.partial(
                bwd_kernel, layer, first, last, tokens, width, count, len(deps)
            ),
            [
                ((rows, (2 if last else 4) * rank), BF),
                ((rows, wide), F32),
                ((rows, wide), F32),
                ((bundle, rank, rank), BF),
                ((bundle, rank, rank), BF),
                ((fan * bundle, rank, rank), BF),
            ],
            *args,
            *deps,
            specs=specs,
            flops=2e9,
        )
        gcur = (g, gd)
        state = reduce_pair(pay)
        stage1[layer] = hop_core(*made)
    made = call(
        functools.partial(end_kernel, width, 0),
        [
            ((heads, rank, rank), BF),
            ((heads, rank, rank), BF),
            ((fan * heads, rank, rank), BF),
        ],
        here,
        *state,
        saves[0],
        *hs[0],
        specs="svvvvv",
        flops=1e8,
    )
    ys = []
    for layer in range(sections):
        if layer not in stage2:
            stage2[layer] = hop_dp(*stage1[layer])
        if layer not in stage3:
            stage3[layer] = hop_far(stage2[layer])
        ys.append(stage3[layer])
    y0 = hop_far(hop_dp(*hop_core(*made)))
    qs = [over_sec(y, 1) for y in ys]
    q0 = over_sec(y0, 1)

    part_down, part_up = call(
        functools.partial(unfold_kernel, scale, sections),
        [((2, rank, cols), F32), ((4, rank, cols), F32)],
        here,
        *ys,
        *qs,
        y0,
        q0,
        *own,
        specs="s" + "a" * (2 * sections + 2) + "vvvv",
        scratch=[
            pltpu.VMEM((bundle, rank, rank), BF),
            pltpu.VMEM((bundle, rank, rank), BF),
            pltpu.VMEM((heads, rank, rank), BF),
            pltpu.VMEM((heads, rank, rank), BF),
            dma((4,)),
        ],
    )
    return (part_down[None], part_up[None])


def solution(mesh):
    in_specs = (
        P("dp", None, None),
        P("dp", None, None),
        P("section", None, None, "dp"),
        P("section", None, None, "dp"),
        P("section", None, None, "dp"),
        P("section", None, None, "dp"),
    )
    out_specs = (P("section", None, None, "dp"), P("section", None, None, "dp"))
    return jax.shard_map(body, mesh=mesh, in_specs=in_specs, out_specs=out_specs, check_vma=False)
```
